32 devices in a mesh: dp: 4 (over y, x), seq: 8 (over z, core).
Axes of the slice: x: 2, y: 2, z: 4, core: 2. Of those that a mesh axis runs over, the one named last changes fastest.
Arguments:
- queries: bfloat16 [4096, 4096], P('seq', 'dp'), may hold values from -6 to 6
- keys: bfloat16 [4096, 4096], P('seq', 'dp'), may hold values from -6 to 6
- values: bfloat16 [4096, 4096], P('seq', 'dp'), may hold values from -6 to 6
- out_grad: bfloat16 [4096, 4096], P('seq', 'dp'), may hold values from -6 to 6
- gain: float32 [4096], P('dp'), may hold values from 0.5 to 1.5
- decay_index: int32 [32], P('dp'), may hold values from 0 to 15
- bounds: int32 [3], replicated, may hold values from 896 to 3200, as said below
Outputs:
- query_grad: bfloat16 [4096, 4096], P('seq', 'dp')
- key_grad: bfloat16 [4096, 4096], P('seq', 'dp')
- value_grad: bfloat16 [4096, 4096], P('seq', 'dp')
- gain_grad: float32 [4096], P(('dp', 'seq'))
The draws below stay inside these ranges and needn't reach their ends.
Inputs may be any that keep to these rules, and one draw needn't show every extreme that they name: `bounds`: the 3 positions rise strictly and lie inside the stream; token p starts a new episode when p is one of them.
All inputs are finite; a program needn't handle non-finite values.
Results may differ from the reference program's by a relative error of at most 0.0063.
Values sent between devices are 32-bit elements; how exact they have to be, the bound alone decides.
A program may use at most 128 MiB of HBM per device.

```python
import jax
import jax.numpy as jnp
from jax import lax

HEADS = 32
HEAD = 128
TOK_DEV = 512
BOUNDS = 3
HD = 4096
SEQ = 4096
N_SEQ = 8


def draw_bounds(key, part):
    spacing = SEQ // (BOUNDS + 1)
    jitter = spacing // 8
    offsets = jax.random.randint(key, (BOUNDS,), -jitter, jitter + 1)
    anchors = (jnp.arange(BOUNDS, dtype=jnp.int32) + 1) * spacing
    return (anchors + offsets).astype(jnp.int32)


def plant(result, rng, least, largest):
    longest = result.shape.index(max(result.shape))
    spots = []
    for shift in (0, 1):
        where = [jax.random.randint(jax.random.fold_in(rng, axis), (), 0, length) for axis, length in enumerate(result.shape)]
        where[longest] = (where[longest] + shift) % result.shape[longest]
        spots.append(tuple(where))
    return result.at[spots[0]].set(least).at[spots[1]].set(largest)


def strengthened(array, rng, source, target, parts, factor):
    owner, partner = [(jnp.arange(array.shape[dim]) // (array.shape[dim] // parts)).reshape([-1 if axis == dim else 1 for axis in range(array.ndim)]) for dim in (source, target)]
    chosen = jax.random.permutation(rng, parts)[partner]
    strong = (owner == chosen) | (owner == (partner + parts // 2) % parts)
    return jnp.where(strong, factor * array, array)


def level_of(own_key, dims, pieces, smallest, top_value):
    factor_of, own = 1.0, jax.random.fold_in(own_key, 6)
    for position, shards_of in pieces:
        heights = jnp.exp(jax.random.uniform(jax.random.fold_in(own, position), (shards_of,), jnp.float32, smallest / len(pieces), top_value / len(pieces)))
        factor_of = factor_of * jnp.repeat(heights, dims[position] // shards_of).reshape([-1 if axis == position else 1 for axis in range(len(dims))])
    return factor_of


def bell_draw(key, dims, deviation, limit, cuts=(), kind=jnp.bfloat16):
    drawn = jax.random.normal(key, dims, jnp.float32) * deviation
    if len(cuts) > 0:
        drawn = level_of(key, dims, cuts, -0.22, 0.18) * drawn
    return jnp.clip(drawn, min=-limit, max=limit).astype(kind)


def gaussian_with(rng, dims, scale, most, pieces, heavy, kind=jnp.bfloat16):
    entries = scale * jax.random.normal(rng, dims, jnp.float32)
    if pieces:
        entries = entries * level_of(rng, dims, pieces, -0.22, 0.18)
    return jnp.clip(strengthened(entries, jax.random.fold_in(rng, 3), *heavy), -most, most).astype(kind)


def setup_inputs(seed: int = 0) -> dict:
    streams_of = jax.random.split(jax.random.key(seed), 8)
    queries = bell_draw(streams_of[0], (SEQ, HD), 1.0, 6.0, ((0, 8), (1, 4)))
    keys = bell_draw(streams_of[1], (SEQ, HD), 1.0, 6.0, ((0, 8), (1, 4)))
    values = bell_draw(streams_of[2], (SEQ, HD), 1.0, 6.0, ((0, 8), (1, 4)))
    out_grad = gaussian_with(streams_of[3], (SEQ, HD), 1.0, 6.0, ((0, 8), (1, 4)), (0, 1, 8, 2.0))
    gain = jnp.clip(1.0 + 0.1 * jax.random.normal(streams_of[4], (HD,), jnp.float32), 0.5, 1.5)
    decay_index = plant(jax.random.randint(streams_of[5], (HEADS,), 0, 16), jax.random.fold_in(streams_of[5], 1), 0, 15).astype(jnp.int32)
    bounds = draw_bounds(jax.random.fold_in(streams_of[7], 71), 0)
    return dict(queries=queries, keys=keys, values=values, out_grad=out_grad, gain=gain, decay_index=decay_index, bounds=bounds)


HIGHEST_PRECISION = lax.Precision.HIGHEST

def decay_rates(decay_index, stream_length):
    level = decay_index.astype(jnp.float32)
    slow_rate = -0.25 * jnp.exp(level / 7.0 * jnp.log(8.0)) / stream_length
    lowest = jnp.log(4.0 / stream_length)
    fast_rate = -jnp.exp(lowest + (level - 8.0) / 7.0 * (jnp.log(1.0 / 32.0) - lowest))
    return jnp.where(decay_index < 8, slow_rate, fast_rate)

def lowered(values_in):
    return lax.optimization_barrier(values_in.astype(jnp.bfloat16)).astype(jnp.float32)

def shard_masks(rates, bound_row, first_row, tok_rows):
    places = first_row + jnp.arange(tok_rows, dtype=jnp.int32)
    episode = lax.optimization_barrier(jnp.sum((bound_row[None, :] <= places[:, None]).astype(jnp.int32), axis=1))
    before = jnp.sum((bound_row <= first_row - 1).astype(jnp.int32))
    enter_mask = (episode == before).astype(jnp.float32)
    leave_mask = (episode == episode[tok_rows - 1]).astype(jnp.float32)
    whole_mask = (episode[tok_rows - 1] == before).astype(jnp.float32)
    local_pos = jnp.arange(tok_rows, dtype=jnp.float32)
    enter_decay = jnp.exp(rates[None, :] * (local_pos[:, None] + 1.0)) * enter_mask[:, None]
    leave_decay = jnp.exp(rates[None, :] * (tok_rows - 1.0 - local_pos[:, None])) * leave_mask[:, None]
    passing_decay = jnp.exp(rates * tok_rows) * whole_mask
    spacing = local_pos[:, None] - local_pos[None, :]
    allowed = (spacing >= 0.0) & (episode[:, None] == episode[None, :])
    weights = jnp.where(allowed[None], jnp.exp(rates[:, None, None] * jnp.maximum(spacing, 0.0)[None]), 0.0)
    return (enter_decay, leave_decay, passing_decay, weights)

def block_grads(query_rows, key_rows, value_rows, grad_rows, gain, masks, state_in, state_grad_end):
    enter_decay, leave_decay, passing_decay, weights = masks
    tok_rows = query_rows.shape[0]
    query_wide = query_rows.astype(jnp.float32)
    key_wide = key_rows.astype(jnp.float32)
    value_wide = value_rows.astype(jnp.float32)
    state_low = lowered(state_in)
    state_grad_low = lowered(state_grad_end)
    scores = jnp.einsum('the,she->hts', query_wide, key_wide, precision=HIGHEST_PRECISION)
    mixing = (scores * weights).astype(jnp.bfloat16)
    attended = jnp.einsum('hts,shf->thf', mixing.astype(jnp.float32), value_wide, precision=HIGHEST_PRECISION)
    attended = attended + enter_decay[:, :, None] * jnp.einsum('the,hef->thf', query_wide, state_low, precision=HIGHEST_PRECISION)
    flat = attended.reshape(tok_rows, -1)
    inverse_rms = lax.rsqrt(lax.optimization_barrier(jnp.mean(flat * flat, axis=1, keepdims=True)) + 1e-06)
    normed = flat * inverse_rms
    grad_wide_in = grad_rows.astype(jnp.float32)
    gained = grad_wide_in * gain[None, :]
    grad_flat = inverse_rms * (gained - normed * lax.optimization_barrier(jnp.mean(gained * normed, axis=1, keepdims=True)))
    grad_mixed = grad_flat.astype(jnp.bfloat16).reshape(query_rows.shape)
    grad_wide = grad_mixed.astype(jnp.float32)
    gain_term = lax.optimization_barrier(jnp.sum(grad_wide_in * normed, axis=0))
    decayed_queries = lowered(enter_decay[:, :, None] * query_wide)
    state_grad_local = jnp.einsum('the,thf->hef', decayed_queries, grad_wide, precision=HIGHEST_PRECISION)
    grad_scores = jnp.einsum('thf,shf->hts', grad_wide, value_wide, precision=HIGHEST_PRECISION)
    grad_mixing = lowered(grad_scores * weights)
    query_grad = jnp.einsum('hts,she->the', grad_mixing, key_wide, precision=HIGHEST_PRECISION)
    query_grad = query_grad + enter_decay[:, :, None] * jnp.einsum('thf,hef->the', grad_wide, state_low, precision=HIGHEST_PRECISION)
    key_grad = jnp.einsum('hts,the->she', grad_mixing, query_wide, precision=HIGHEST_PRECISION)
    key_grad = key_grad + leave_decay[:, :, None] * jnp.einsum('thf,hef->the', value_wide, state_grad_low, precision=HIGHEST_PRECISION)
    value_grad = jnp.einsum('hts,thf->shf', mixing.astype(jnp.float32), grad_wide, precision=HIGHEST_PRECISION)
    value_grad = value_grad + leave_decay[:, :, None] * jnp.einsum('the,hef->thf', key_wide, state_grad_low, precision=HIGHEST_PRECISION)
    return (query_grad, key_grad, value_grad, gain_term, state_grad_local)

def reference(queries, keys, values, out_grad, gain, decay_index, bounds):
    rates = decay_rates(decay_index, float(SEQ))
    starts = jnp.arange(N_SEQ, dtype=jnp.int32) * TOK_DEV
    shape_four = (N_SEQ, TOK_DEV, HEADS, HEAD)
    query_all = queries.reshape(shape_four)
    key_all = keys.reshape(shape_four)
    value_all = values.reshape(shape_four)
    grad_all = out_grad.reshape(N_SEQ, TOK_DEV, HD)
    zero_state = jnp.zeros((HEADS, HEAD, HEAD), jnp.float32)

    def forward(state_in, block):
        key_rows, value_rows, first_row = block
        masks = shard_masks(rates, bounds, first_row, TOK_DEV)
        decayed_keys = lowered(masks[1][:, :, None] * key_rows.astype(jnp.float32))
        state_local = jnp.einsum('the,thf->hef', decayed_keys, value_rows.astype(jnp.float32), precision=HIGHEST_PRECISION)
        return (masks[2][:, None, None] * state_in + state_local, state_in)
    unused, states_in = lax.scan(forward, zero_state, (key_all, value_all, starts))

    def backward(state_grad_end, block):
        query_rows, key_rows, value_rows, grad_rows, first_row, state_in = block
        masks = shard_masks(rates, bounds, first_row, TOK_DEV)
        query_grad, key_grad, value_grad, gain_term, state_grad_local = block_grads(query_rows, key_rows, value_rows, grad_rows, gain, masks, state_in, state_grad_end)
        carried = state_grad_local + masks[2][:, None, None] * state_grad_end
        return (carried, (query_grad.astype(jnp.bfloat16), key_grad.astype(jnp.bfloat16), value_grad.astype(jnp.bfloat16), gain_term))
    unused_end, outputs = lax.scan(backward, zero_state, (query_all, key_all, value_all, grad_all, starts, states_in), reverse=True)
    query_grad, key_grad, value_grad, gain_terms = outputs
    return (query_grad.reshape(SEQ, HD), key_grad.reshape(SEQ, HD), value_grad.reshape(SEQ, HD), lax.optimization_barrier(jnp.sum(gain_terms, axis=0)))
```

```python
import functools
import math

import jax
import jax.numpy as jnp
from jax import lax
from jax.experimental import pallas as pl
from jax.experimental.pallas import tpu as pltpu
from jax.sharding import PartitionSpec as P

MESH = pl.DeviceIdType.MESH
F32, BF16 = jnp.float32, jnp.bfloat16
FAR = 1e30
CHUNKS = 2
HEADS_PER_HOP = 2

NN = (((1,), (0,)), ((), ()))
NT = (((1,), (1,)), ((), ()))
TN = (((0,), (0,)), ((), ()))


def dot(a, b, dims):
    return lax.dot_general(a, b, dims, preferred_element_type=F32)


def kernel(
    cfg,
    q_ref, k_ref, v_ref, g_ref, gain_ref, dec_ref, bounds_ref,
    dq_ref, dk_ref, dv_ref, gg_ref,
    rate_ref, pass_ref, enter_ref, leave_ref, dist_ref,
    mix_ref, o_ref, do_ref, dki_ref, dvi_ref, low_ref, dlow_ref,
    sq_ref, cr_ref, stat_ref, gsrc_ref, grecv_ref,
    f_ls, f_lo, f_lr, f_x, f_xs, f_ss, f_sr,
    b_ls, b_lo, b_lr, b_x, b_xs, b_ss, b_sr,
    f_l_sem, f_x_sem, f_s_sem, b_l_sem, b_x_sem, b_s_sem, stat_sem, gain_sem,
):
    tok, heads, size, n_seq, n_dp, scatter = cfg
    half, mid = heads // 2, tok // 2
    rows = size // CHUNKS
    pos, dpi = lax.axis_index("seq"), lax.axis_index("dp")
    core, chip = lax.rem(pos, 2), lax.div(pos, 2)
    chips = n_seq // 2
    partner = chip * 2 + 1 - core
    barrier = pltpu.get_barrier_semaphore()

    def greet(axis, mine):
        def body(j, carry):
            @pl.when(j != mine)
            def _():
                pl.semaphore_signal(barrier, inc=1, device_id={axis: j}, device_id_type=MESH)

            return carry

        return body

    lax.fori_loop(0, n_seq, greet("seq", pos), 0)
    lax.fori_loop(0, n_dp, greet("dp", dpi), 0)

    def cols(h):
        return pl.ds(pl.multiple_of(h * size, size), size)

    def episode(place):
        total = 0
        for b in range(bounds_ref.shape[0]):
            total = total + (bounds_ref[b] <= place).astype(jnp.int32)
        return total

    first = pos * tok
    line = lax.broadcasted_iota(jnp.int32, (heads, tok), 0)
    level_int = jnp.zeros((heads, tok), jnp.int32)
    for h in range(heads):
        level_int = jnp.where(line == h, dec_ref[h], level_int)
    level = level_int.astype(F32)
    stream = float(tok * n_seq)
    lowest = math.log(4.0 / stream)
    slow = -0.25 * jnp.exp(level / 7.0 * math.log(8.0)) / stream
    fast = -jnp.exp(lowest + (level - 8.0) / 7.0 * (math.log(1.0 / 32.0) - lowest))
    rates = jnp.where(level_int < 8, slow, fast)
    for h in range(heads):
        rate_ref[h] = rates[h : h + 1]
    for c in range(2):
        start = (chip * 2 + c) * tok
        whole = (episode(start + tok - 1) == episode(start - 1)).astype(F32)
        passing = jnp.exp(rates[:, :size] * float(tok)) * whole
        for h in range(heads):
            pass_ref[c, h] = passing[h : h + 1]
    t_col = lax.broadcasted_iota(jnp.int32, (tok, size), 0)
    e_col = episode(first + t_col)
    t_val = t_col.astype(F32)
    enter_ref[...] = jnp.where(e_col == episode(first - 1), t_val + 1.0, FAR)
    leave_ref[...] = jnp.where(e_col == episode(first + tok - 1), tok - 1.0 - t_val, FAR)

    def decay(h, where_ref):
        return jnp.exp(rate_ref[h][:, :size] * where_ref[...])

    def local_state(h, a_ref, where_ref, b_ref):
        scaled = (decay(h, where_ref) * a_ref[:, cols(h)].astype(F32)).astype(BF16)
        return dot(scaled, b_ref[:, cols(h)], TN)

    theirs, own = (1 - core) * half, core * half

    def remote(src, dst, send, recv, target):
        return pltpu.make_async_remote_copy(
            src_ref=src, dst_ref=dst, send_sem=send, recv_sem=recv,
            device_id=target, device_id_type=MESH,
        )

    def l_copy(bufs, sem, i):
        return remote(bufs[0].at[i], bufs[2].at[i], sem.at[0, i], sem.at[1, i], {"seq": partner})

    def x_copy(bufs, sem, i, r, step):
        part = pl.ds(r * rows, rows)
        return remote(
            bufs[4].at[i, part], bufs[3].at[i, part],
            sem.at[0, i * CHUNKS + r], sem.at[1, i * CHUNKS + r], {"seq": pos + 2 * step},
        )

    def s_copy(bufs, sem, i, r):
        part = pl.ds(r * rows, rows)
        return remote(
            bufs[5].at[i, part], bufs[6].at[i, part],
            sem.at[0, i * CHUNKS + r], sem.at[1, i * CHUNKS + r], {"seq": partner},
        )

    def chain(bufs, l_sem, x_sem, s_sem, step, target_ref):
        if step > 0:
            rel, has_up, has_down = core, chip > 0, chip < chips - 1
            near, distant = 0, 1
        else:
            rel, has_up, has_down = 1 - core, chip < chips - 1, chip > 0
            near, distant = 1, 0
        lo, lr, x_in, xs, ss = bufs[1], bufs[2], bufs[3], bufs[4], bufs[5]
        is_near = rel == 0

        def body(i, carry):
            h = own + i
            l_copy(bufs, l_sem, i).wait_recv()
            pa = pass_ref[near, h]
            pb = pass_ref[distant, h]
            for r in range(CHUNKS):
                part = pl.ds(r * rows, rows)

                @pl.when(has_up)
                def _():
                    x_copy(bufs, x_sem, i, r, step).wait_recv()

                @pl.when(jnp.logical_not(has_up))
                def _():
                    x_in[i, part, :] = jnp.zeros((rows, size), F32)

                x, mine, other = x_in[i, part, :], lo[i, part, :], lr[i, part, :]
                la, lb = jnp.where(is_near, mine, other), jnp.where(is_near, other, mine)
                after = pa * x + la
                xs[i, part, :] = pb * after + lb

                @pl.when(has_down)
                def _():
                    x_copy(bufs, x_sem, i, r, step).start()

                ss[i, part, :] = jnp.where(is_near, after, x)
                s_copy(bufs, s_sem, i, r).start()
                target_ref[h, part, :] = jnp.where(is_near, x, after).astype(BF16)
            return carry

        lax.fori_loop(0, half, body, 0)

        return has_down

    def take_partner(bufs, s_sem, target_ref, i):
        for r in range(CHUNKS):
            s_copy(bufs, s_sem, i, r).wait_recv()
        target_ref[theirs + i] = bufs[6][i].astype(BF16)

    def finish(bufs, l_sem, x_sem, s_sem, step, has_down):
        def body(i, carry):
            l_copy(bufs, l_sem, i).wait_send()
            for r in range(CHUNKS):
                s_copy(bufs, s_sem, i, r).wait_send()

                @pl.when(has_down)
                def _():
                    x_copy(bufs, x_sem, i, r, step).wait_send()

            return carry

        lax.fori_loop(0, half, body, 0)

    fwd = (f_ls, f_lo, f_lr, f_x, f_xs, f_ss, f_sr)
    bwd = (b_ls, b_lo, b_lr, b_x, b_xs, b_ss, b_sr)

    def fwd_theirs(i, carry):
        f_ls[i] = local_state(theirs + i, k_ref, leave_ref, v_ref)
        return carry

    lax.fori_loop(0, half, fwd_theirs, 0)
    pl.semaphore_wait(barrier, n_seq - 1 + n_dp - 1)

    def fwd_own(i, carry):
        l_copy(fwd, f_l_sem, i).start()
        f_lo[i] = local_state(own + i, k_ref, leave_ref, v_ref)
        return carry

    lax.fori_loop(0, half, fwd_own, 0)

    t_full = lax.broadcasted_iota(jnp.int32, (tok, tok), 0)
    s_full = lax.broadcasted_iota(jnp.int32, (tok, tok), 1)
    e_row = episode(first + lax.broadcasted_iota(jnp.int32, (1, tok), 1))
    e_tall = episode(first + lax.broadcasted_iota(jnp.int32, (tok, 1), 0))
    allowed = (t_full >= s_full) & (e_row == e_tall)
    early, late = pl.ds(0, mid), pl.ds(mid, mid)

    def weights(h):
        rate = rate_ref[h]
        top = jnp.exp(rate[:, :mid] * dist_ref[0:mid, 0:mid])
        low = jnp.exp(rate * dist_ref[mid:tok, :])
        return top, low

    def intra(h, carry):
        c = cols(h)
        top, low = weights(h)
        k_all = k_ref[:, c]
        a_top = (dot(q_ref[early, c], k_ref[early, c], NT) * top).astype(BF16)
        a_low = (dot(q_ref[late, c], k_all, NT) * low).astype(BF16)
        mix_ref[h, 0:mid, 0:mid] = a_top
        mix_ref[h, mid:tok, :] = a_low
        o_ref[early, c] = dot(a_top, v_ref[early, c], NN)
        o_ref[late, c] = dot(a_low, v_ref[:, c], NN)
        return carry

    f_before = jnp.minimum(chip * HEADS_PER_HOP, heads)
    dist_ref[...] = jnp.where(allowed, (t_full - s_full).astype(F32), FAR)
    lax.fori_loop(0, f_before, intra, 0)
    f_down = chain(fwd, f_l_sem, f_x_sem, f_s_sem, 1, low_ref)
    lax.fori_loop(f_before, heads, intra, 0)

    sq_ref[...] = jnp.zeros_like(sq_ref)
    cr_ref[...] = jnp.zeros_like(cr_ref)

    def outputs(h):
        c = cols(h)
        o = o_ref[:, c] + decay(h, enter_ref) * dot(q_ref[:, c], low_ref[h], NN)
        o_ref[:, c] = o
        sq_ref[...] += o * o
        cr_ref[...] += g_ref[:, c].astype(F32) * gain_ref[pl.ds(h, 1), :] * o

    def out_own(i, carry):
        outputs(own + i)
        return carry

    def out_theirs(i, carry):
        take_partner(fwd, f_s_sem, low_ref, i)
        outputs(theirs + i)
        return carry

    lax.fori_loop(0, half, out_own, 0)
    lax.fori_loop(0, half, out_theirs, 0)

    sq_row = jnp.sum(jnp.transpose(sq_ref[...]), axis=0, keepdims=True)
    cr_row = jnp.sum(jnp.transpose(cr_ref[...]), axis=0, keepdims=True)
    line8 = lax.broadcasted_iota(jnp.int32, (8, tok), 0)
    stat_ref[dpi] = jnp.where(line8 == 0, sq_row, jnp.where(line8 == 1, cr_row, 0.0))

    def stat_copy(j, slot):
        return remote(
            stat_ref.at[slot], stat_ref.at[slot], stat_sem.at[0, j], stat_sem.at[1, slot],
            {"dp": j},
        )

    def stat_send(j, carry):
        @pl.when(j != dpi)
        def _():
            stat_copy(j, dpi).start()

        return carry

    def stat_recv(j, carry):
        @pl.when(j != dpi)
        def _():
            stat_copy(j, j).wait_recv()

        return carry

    def stat_done(j, carry):
        @pl.when(j != dpi)
        def _():
            stat_copy(j, dpi).wait_send()

        return carry

    lax.fori_loop(0, n_dp, stat_send, 0)
    lax.fori_loop(0, n_dp, stat_recv, 0)
    total = stat_ref[0]
    for j in range(1, n_dp):
        total = total + stat_ref[j]
    features = float(heads * size * n_dp)
    inv_row = lax.rsqrt(total[0:1, :] / features + 1e-06)
    mean_row = inv_row * total[1:2, :] / features
    sq_ref[...] = jnp.transpose(jnp.broadcast_to(inv_row, (size, tok)))
    cr_ref[...] = jnp.transpose(jnp.broadcast_to(mean_row, (size, tok)))

    def norm_grad(h):
        c = cols(h)
        inv = sq_ref[...]
        grad = g_ref[:, c].astype(F32)
        normed = inv * o_ref[:, c]
        do_ref[:, c] = (inv * (grad * gain_ref[pl.ds(h, 1), :] - normed * cr_ref[...])).astype(BF16)
        gsrc_ref[h] = jnp.sum((grad * normed).reshape(tok // 8, 8, size), axis=0)

    def bwd_theirs(i, carry):
        norm_grad(theirs + i)
        b_ls[i] = local_state(theirs + i, q_ref, enter_ref, do_ref)
        l_copy(bwd, b_l_sem, i).start()
        return carry

    def bwd_own(i, carry):
        norm_grad(own + i)
        b_lo[i] = local_state(own + i, q_ref, enter_ref, do_ref)
        return carry

    lax.fori_loop(0, half, bwd_theirs, 0)
    lax.fori_loop(0, half, bwd_own, 0)

    def gain_copy(j, slot):
        return remote(
            gsrc_ref.at[j], grecv_ref.at[slot], gain_sem.at[0, j], gain_sem.at[1, slot],
            {"seq": j},
        )

    def gain_send(j, carry):
        @pl.when(j != pos)
        def _():
            gain_copy(j, pos).start()

        return carry

    def gain_recv(j, carry):
        @pl.when(j != pos)
        def _():
            gain_copy(j, j).wait_recv()
            gain_copy(j, pos).wait_send()

        return carry

    def intra_grad(h, carry):
        c = cols(h)
        top, low = weights(h)
        q0, q1 = q_ref[early, c], q_ref[late, c]
        d0, d1 = do_ref[early, c], do_ref[late, c]
        da_top = (dot(d0, v_ref[early, c], NT) * top).astype(BF16)
        da_low = (dot(d1, v_ref[:, c], NT) * low).astype(BF16)
        enter = decay(h, enter_ref)
        state = low_ref[h]
        dq_ref[early, c] = (
            dot(da_top, k_ref[early, c], NN) + enter[:mid] * dot(d0, state, NT)
        ).astype(BF16)
        dq_ref[late, c] = (
            dot(da_low, k_ref[:, c], NN) + enter[mid:] * dot(d1, state, NT)
        ).astype(BF16)
        dki_ref[early, c] = dot(da_top, q0, TN) + dot(da_low[:, :mid], q1, TN)
        dki_ref[late, c] = dot(da_low[:, mid:], q1, TN)
        dvi_ref[early, c] = dot(mix_ref[h, 0:mid, 0:mid], d0, TN) + dot(
            mix_ref[h, mid:tok, 0:mid], d1, TN
        )
        dvi_ref[late, c] = dot(mix_ref[h, mid:tok, mid:tok], d1, TN)
        return carry

    b_before = jnp.minimum((chips - 1 - chip) * HEADS_PER_HOP, heads)
    lax.fori_loop(0, b_before, intra_grad, 0)
    b_down = chain(bwd, b_l_sem, b_x_sem, b_s_sem, -1, dlow_ref)
    if scatter:
        lax.fori_loop(0, n_seq, gain_send, 0)
    lax.fori_loop(b_before, heads, intra_grad, 0)

    def final(h):
        c = cols(h)
        leave = decay(h, leave_ref)
        state = dlow_ref[h]
        dk_ref[:, c] = (dki_ref[:, c] + leave * dot(v_ref[:, c], state, NT)).astype(BF16)
        dv_ref[:, c] = (dvi_ref[:, c] + leave * dot(k_ref[:, c], state, NN)).astype(BF16)

    def final_own(i, carry):
        final(own + i)
        return carry

    def final_theirs(i, carry):
        take_partner(bwd, b_s_sem, dlow_ref, i)
        final(theirs + i)
        return carry

    lax.fori_loop(0, half, final_own, 0)
    lax.fori_loop(0, half, final_theirs, 0)

    if scatter:
        grecv_ref[pos] = gsrc_ref[pos]
        lax.fori_loop(0, n_seq, gain_recv, 0)
        gain_sum = grecv_ref[0]
        for j in range(1, n_seq):
            gain_sum = gain_sum + grecv_ref[j]
        gg_ref[...] = jnp.sum(gain_sum, axis=0, keepdims=True)
    else:
        for h in range(heads):
            gg_ref[h : h + 1, :] = jnp.sum(gsrc_ref[h], axis=0, keepdims=True)
    finish(fwd, f_l_sem, f_x_sem, f_s_sem, 1, f_down)
    finish(bwd, b_l_sem, b_x_sem, b_s_sem, -1, b_down)
    lax.fori_loop(0, n_dp, stat_done, 0)


def shards(queries, keys, values, out_grad, gain, decay_index, bounds):
    tok, width = queries.shape
    heads = decay_index.shape[0]
    size = width // heads
    n_seq, n_dp = lax.axis_size("seq"), lax.axis_size("dp")
    half = heads // 2
    scatter = n_seq == heads
    cfg = (tok, heads, size, n_seq, n_dp, scatter)
    vmem = pl.BlockSpec(memory_space=pltpu.VMEM)
    smem = pl.BlockSpec(memory_space=pltpu.SMEM)
    state = pltpu.VMEM((half, size, size), F32)
    dma = pltpu.SemaphoreType.DMA
    chain_sems = [dma((2, half)), dma((2, half * CHUNKS)), dma((2, half * CHUNKS))]
    grads = jax.ShapeDtypeStruct((tok, width), BF16)
    query_grad, key_grad, value_grad, gain_part = pl.pallas_call(
        functools.partial(kernel, cfg),
        out_shape=[
            grads,
            grads,
            grads,
            jax.ShapeDtypeStruct((1 if scatter else heads, size), F32),
        ],
        in_specs=[vmem] * 5 + [smem] * 2,
        out_specs=[vmem] * 4,
        scratch_shapes=[
            pltpu.VMEM((heads, 1, tok), F32),
            pltpu.VMEM((2, heads, 1, size), F32),
            pltpu.VMEM((tok, size), F32),
            pltpu.VMEM((tok, size), F32),
            pltpu.VMEM((tok, tok), F32),
            pltpu.VMEM((heads, tok, tok), BF16),
            pltpu.VMEM((tok, width), F32),
            pltpu.VMEM((tok, width), BF16),
            pltpu.VMEM((tok, width), F32),
            pltpu.VMEM((tok, width), F32),
            pltpu.VMEM((heads, size, size), BF16),
            pltpu.VMEM((heads, size, size), BF16),
            pltpu.VMEM((tok, size), F32),
            pltpu.VMEM((tok, size), F32),
            pltpu.VMEM((n_dp, 8, tok), F32),
            pltpu.VMEM((heads, 8, size), F32),
            pltpu.VMEM((n_seq, 8, size), F32),
        ]
        + [state] * 14
        + chain_sems * 2
        + [dma((2, n_dp)), dma((2, n_seq))],
        compiler_params=pltpu.CompilerParams(
            collective_id=0, has_side_effects=True, vmem_limit_bytes=60 * 1024 * 1024
        ),
    )(queries, keys, values, out_grad, gain.reshape(heads, size), decay_index, bounds)
    if scatter:
        gain_grad = gain_part.reshape(-1)
    else:
        gain_grad = lax.psum_scatter(
            gain_part.reshape(-1), "seq", scatter_dimension=0, tiled=True
        )
    return query_grad, key_grad, value_grad, gain_grad


def solution(mesh):
    return jax.shard_map(
        shards,
        mesh=mesh,
        in_specs=(
            P("seq", "dp"),
            P("seq", "dp"),
            P("seq", "dp"),
            P("seq", "dp"),
            P("dp"),
            P("dp"),
            P(),
        ),
        out_specs=(P("seq", "dp"), P("seq", "dp"), P("seq", "dp"), P(("dp", "seq"))),
        check_vma=False,
    )
```

```python
import functools
import math

import jax
import jax.numpy as jnp
from jax import lax
from jax.experimental import pallas as pl
from jax.experimental.pallas import tpu as pltpu
from jax.sharding import PartitionSpec as P

MESH = pl.DeviceIdType.MESH
F32, BF16 = jnp.float32, jnp.bfloat16
FAR = 1e30
CHUNKS = 4
FWD_PER_HOP = 4
BWD_PER_HOP = 3
FINAL_HEADS = 4

NN = (((1,), (0,)), ((), ()))
NT = (((1,), (1,)), ((), ()))
TN = (((0,), (0,)), ((), ()))


def dot(a, b, dims):
    return lax.dot_general(a, b, dims, preferred_element_type=F32)


def decay_rates(level_int, stream):
    level = level_int.astype(F32)
    lowest = math.log(4.0 / stream)
    slow = -0.25 * jnp.exp(level / 7.0 * math.log(8.0)) / stream
    fast = -jnp.exp(lowest + (level - 8.0) / 7.0 * (math.log(1.0 / 32.0) - lowest))
    return jnp.where(level_int < 8, slow, fast)


def episode_of(bounds_ref, place):
    total = 0
    for b in range(bounds_ref.shape[0]):
        total = total + (bounds_ref[b] <= place).astype(jnp.int32)
    return total


def final_kernel(
    cfg, dec_ref, bounds_ref, k_ref, v_ref, dqi_ref, dki_ref, dvi_ref, dlow_ref, ggi_ref,
    dq_ref, dk_ref, dv_ref, gg_ref,
):
    tok, size, n_seq = cfg
    first = lax.axis_index("seq") * tok
    t_col = lax.broadcasted_iota(jnp.int32, (tok, size), 0)
    same = episode_of(bounds_ref, first + t_col) == episode_of(bounds_ref, first + tok - 1)
    leave_pos = jnp.where(same, tok - 1.0 - t_col.astype(F32), FAR)
    dq_ref[...] = dqi_ref[...]
    gg_ref[...] = ggi_ref[...]
    for u in range(FINAL_HEADS):
        level = jnp.full((1, size), dec_ref[pl.program_id(0) * FINAL_HEADS + u], jnp.int32)
        leave = jnp.exp(decay_rates(level, float(tok * n_seq)) * leave_pos)
        c = slice(u * size, (u + 1) * size)
        state = dlow_ref[u]
        dk_ref[:, c] = (dki_ref[:, c].astype(F32) + leave * dot(v_ref[:, c], state, NT)).astype(BF16)
        dv_ref[:, c] = (dvi_ref[:, c].astype(F32) + leave * dot(k_ref[:, c], state, NN)).astype(BF16)


def kernel(
    cfg,
    q_hbm, k_hbm, v_hbm, g_hbm, gain_ref, dec_ref, bounds_ref,
    dq_hbm, dki_hbm, dvi_hbm, dlow_hbm, gg_ref,
    q_ref, k_ref, v_ref, g_ref, dq_ref,
    rate_ref, pass_ref, enter_ref, leave_ref, dist_ref,
    mix_ref, o_ref, do_ref, dki_ref, dvi_ref, low_ref, dlow_ref,
    sq_ref, cr_ref, stat_ref, gsrc_ref, grecv_ref,
    f_ls, f_lo, f_lr, f_x, f_xs, f_ss, f_sr,
    b_ls, b_lo, b_lr, b_x, b_xs, b_ss, b_sr,
    f_l_sem, f_x_sem, f_s_sem, b_l_sem, b_x_sem, b_s_sem, stat_sem, gain_sem,
    in_sem, out_sem,
):
    tok, heads, size, n_seq, n_dp, scatter = cfg
    half, mid = heads // 2, tok // 2
    rows = size // CHUNKS
    pos, dpi = lax.axis_index("seq"), lax.axis_index("dp")
    core, chip = lax.rem(pos, 2), lax.div(pos, 2)
    chips = n_seq // 2
    partner = chip * 2 + 1 - core
    loads = [
        pltpu.make_async_copy(src, dst, in_sem.at[i])
        for i, (src, dst) in enumerate(
            ((k_hbm, k_ref), (v_hbm, v_ref), (q_hbm, q_ref), (g_hbm, g_ref))
        )
    ]
    for load in loads:
        load.start()
    barrier = pltpu.get_barrier_semaphore()

    def greet(axis, mine):
        def body(j, carry):
            @pl.when(j != mine)
            def _():
                pl.semaphore_signal(barrier, inc=1, device_id={axis: j}, device_id_type=MESH)

            return carry

        return body

    lax.fori_loop(0, n_seq, greet("seq", pos), 0)
    lax.fori_loop(0, n_dp, greet("dp", dpi), 0)

    def cols(h):
        return pl.ds(pl.multiple_of(h * size, size), size)

    def episode(place):
        return episode_of(bounds_ref, place)

    first = pos * tok
    line = lax.broadcasted_iota(jnp.int32, (heads, tok), 0)
    level_int = jnp.zeros((heads, tok), jnp.int32)
    for h in range(heads):
        level_int = jnp.where(line == h, dec_ref[h], level_int)
    rates = decay_rates(level_int, float(tok * n_seq))
    for h in range(heads):
        rate_ref[h] = rates[h : h + 1]
    for c in range(2):
        start = (chip * 2 + c) * tok
        whole = (episode(start + tok - 1) == episode(start - 1)).astype(F32)
        passing = jnp.exp(rates[:, :size] * float(tok)) * whole
        for h in range(heads):
            pass_ref[c, h] = passing[h : h + 1]
    t_col = lax.broadcasted_iota(jnp.int32, (tok, size), 0)
    e_col = episode(first + t_col)
    t_val = t_col.astype(F32)
    enter_ref[...] = jnp.where(e_col == episode(first - 1), t_val + 1.0, FAR)
    leave_ref[...] = jnp.where(e_col == episode(first + tok - 1), tok - 1.0 - t_val, FAR)

    def decay(h, where_ref):
        return jnp.exp(rate_ref[h][:, :size] * where_ref[...])

    def local_state(h, a_ref, where_ref, b_ref):
        scaled = (decay(h, where_ref) * a_ref[:, cols(h)].astype(F32)).astype(BF16)
        return dot(scaled, b_ref[:, cols(h)], TN)

    theirs, own = (1 - core) * half, core * half

    def remote(src, dst, send, recv, target):
        return pltpu.make_async_remote_copy(
            src_ref=src, dst_ref=dst, send_sem=send, recv_sem=recv,
            device_id=target, device_id_type=MESH,
        )

    def l_copy(bufs, sem, i):
        return remote(bufs[0].at[i], bufs[2].at[i], sem.at[0, i], sem.at[1, i], {"seq": partner})

    def x_copy(bufs, sem, i, r, step):
        part = pl.ds(r * rows, rows)
        return remote(
            bufs[4].at[i, part], bufs[3].at[i, part],
            sem.at[0, i * CHUNKS + r], sem.at[1, i * CHUNKS + r], {"seq": pos + 2 * step},
        )

    def s_copy(bufs, sem, i, r):
        part = pl.ds(r * rows, rows)
        return remote(
            bufs[5].at[i, part], bufs[6].at[i, part],
            sem.at[0, i * CHUNKS + r], sem.at[1, i * CHUNKS + r], {"seq": partner},
        )

    def direction(step):
        if step > 0:
            return core, chip > 0, chip < chips - 1
        return 1 - core, chip < chips - 1, chip > 0

    def chain_step(bufs, sems, step, target_ref, i):
        rel, has_up, has_down = direction(step)
        near, distant = (0, 1) if step > 0 else (1, 0)
        l_sem, x_sem, s_sem = sems
        lo, lr, x_in, xs, ss = bufs[1], bufs[2], bufs[3], bufs[4], bufs[5]
        is_near = rel == 0
        h = own + i
        l_copy(bufs, l_sem, i).wait_recv()
        pa, pb = pass_ref[near, h], pass_ref[distant, h]
        for r in range(CHUNKS):
            part = pl.ds(r * rows, rows)

            @pl.when(has_up)
            def _():
                x_copy(bufs, x_sem, i, r, step).wait_recv()

            @pl.when(jnp.logical_not(has_up))
            def _():
                x_in[i, part, :] = jnp.zeros((rows, size), F32)

            x, mine, other = x_in[i, part, :], lo[i, part, :], lr[i, part, :]
            la, lb = jnp.where(is_near, mine, other), jnp.where(is_near, other, mine)
            after = pa * x + la
            xs[i, part, :] = pb * after + lb

            @pl.when(has_down)
            def _():
                x_copy(bufs, x_sem, i, r, step).start()

            ss[i, part, :] = jnp.where(is_near, after, x)
            s_copy(bufs, s_sem, i, r).start()
            target_ref[h, part, :] = jnp.where(is_near, x, after).astype(BF16)

    def take_partner(bufs, s_sem, target_ref, i):
        for r in range(CHUNKS):
            s_copy(bufs, s_sem, i, r).wait_recv()
        target_ref[theirs + i] = bufs[6][i].astype(BF16)

    def finish(bufs, sems, step):
        l_sem, x_sem, s_sem = sems
        has_down = direction(step)[2]

        def body(i, carry):
            l_copy(bufs, l_sem, i).wait_send()
            for r in range(CHUNKS):
                s_copy(bufs, s_sem, i, r).wait_send()

                @pl.when(has_down)
                def _():
                    x_copy(bufs, x_sem, i, r, step).wait_send()

            return carry

        lax.fori_loop(0, half, body, 0)

    fwd = (f_ls, f_lo, f_lr, f_x, f_xs, f_ss, f_sr)
    bwd = (b_ls, b_lo, b_lr, b_x, b_xs, b_ss, b_sr)

    fwd_sems = (f_l_sem, f_x_sem, f_s_sem)
    bwd_sems = (b_l_sem, b_x_sem, b_s_sem)

    f_head, b_head = chip == 0, chip == chips - 1
    loads[0].wait()
    loads[1].wait()
    pl.semaphore_wait(barrier, n_seq - 1 + n_dp - 1)
    for i in range(half):
        f_ls[i] = local_state(theirs + i, k_ref, leave_ref, v_ref)
        l_copy(fwd, f_l_sem, i).start()
        f_lo[i] = local_state(own + i, k_ref, leave_ref, v_ref)
        if i > 0:

            @pl.when(f_head)
            def _():
                chain_step(fwd, fwd_sems, 1, low_ref, i - 1)

    @pl.when(f_head)
    def _():
        chain_step(fwd, fwd_sems, 1, low_ref, half - 1)

    loads[2].wait()
    loads[3].wait()

    t_full = lax.broadcasted_iota(jnp.int32, (tok, tok), 0)
    s_full = lax.broadcasted_iota(jnp.int32, (tok, tok), 1)
    e_row = episode(first + lax.broadcasted_iota(jnp.int32, (1, tok), 1))
    e_tall = episode(first + lax.broadcasted_iota(jnp.int32, (tok, 1), 0))
    allowed = (t_full >= s_full) & (e_row == e_tall)
    early, late = pl.ds(0, mid), pl.ds(mid, mid)

    def weights(h):
        rate = rate_ref[h]
        top = jnp.exp(rate[:, :mid] * dist_ref[0:mid, 0:mid])
        low = jnp.exp(rate * dist_ref[mid:tok, :])
        return top, low

    def intra(h, carry):
        c = cols(h)
        top, low = weights(h)
        k_all = k_ref[:, c]
        a_top = (dot(q_ref[early, c], k_ref[early, c], NT) * top).astype(BF16)
        a_low = (dot(q_ref[late, c], k_all, NT) * low).astype(BF16)
        mix_ref[h, 0:mid, 0:mid] = a_top
        mix_ref[h, mid:tok, :] = a_low
        o_ref[early, c] = dot(a_top, v_ref[early, c], NN)
        o_ref[late, c] = dot(a_low, v_ref[:, c], NN)
        return carry

    f_before = jnp.minimum(chip * FWD_PER_HOP, heads)
    f_full = f_before >= heads
    dist_ref[...] = jnp.where(allowed, (t_full - s_full).astype(F32), FAR)
    lax.fori_loop(0, f_before, intra, 0)

    sq_ref[...] = jnp.zeros_like(sq_ref)
    cr_ref[...] = jnp.zeros_like(cr_ref)

    def outputs(h):
        c = cols(h)
        o = o_ref[:, c] + decay(h, enter_ref) * dot(q_ref[:, c], low_ref[h], NN)
        o_ref[:, c] = o
        sq_ref[...] += o * o
        cr_ref[...] += g_ref[:, c].astype(F32) * gain_ref[pl.ds(h, 1), :] * o

    def out_own(i, carry):
        outputs(own + i)
        return carry

    def out_theirs(i, carry):
        take_partner(fwd, f_s_sem, low_ref, i)
        outputs(theirs + i)
        return carry

    def fwd_chain(i, carry):
        chain_step(fwd, fwd_sems, 1, low_ref, i)

        @pl.when(f_full)
        def _():
            out_own(i, 0)

        @pl.when(f_full & (i > 0))
        def _():
            out_theirs(i - 1, 0)

        return carry

    lax.fori_loop(jnp.where(f_head, half, 0), half, fwd_chain, 0)
    lax.fori_loop(f_before, heads, intra, 0)
    lax.fori_loop(jnp.where(f_full, half, 0), half, out_own, 0)
    lax.fori_loop(jnp.where(f_full, half - 1, 0), half, out_theirs, 0)

    sq_row = jnp.sum(jnp.transpose(sq_ref[...]), axis=0, keepdims=True)
    cr_row = jnp.sum(jnp.transpose(cr_ref[...]), axis=0, keepdims=True)
    line8 = lax.broadcasted_iota(jnp.int32, (8, tok), 0)
    stat_ref[dpi] = jnp.where(line8 == 0, sq_row, jnp.where(line8 == 1, cr_row, 0.0))

    def stat_copy(j, slot):
        return remote(
            stat_ref.at[slot], stat_ref.at[slot], stat_sem.at[0, j], stat_sem.at[1, slot],
            {"dp": j},
        )

    def stat_send(j, carry):
        @pl.when(j != dpi)
        def _():
            stat_copy(j, dpi).start()

        return carry

    def stat_recv(j, carry):
        @pl.when(j != dpi)
        def _():
            stat_copy(j, j).wait_recv()

        return carry

    def stat_done(j, carry):
        @pl.when(j != dpi)
        def _():
            stat_copy(j, dpi).wait_send()

        return carry

    lax.fori_loop(0, n_dp, stat_send, 0)
    lax.fori_loop(0, n_dp, stat_recv, 0)
    total = stat_ref[0]
    for j in range(1, n_dp):
        total = total + stat_ref[j]
    features = float(heads * size * n_dp)
    inv_row = lax.rsqrt(total[0:1, :] / features + 1e-06)
    mean_row = inv_row * total[1:2, :] / features
    sq_ref[...] = jnp.transpose(jnp.broadcast_to(inv_row, (size, tok)))
    cr_ref[...] = jnp.transpose(jnp.broadcast_to(mean_row, (size, tok)))

    def norm_grad(h):
        c = cols(h)
        inv = sq_ref[...]
        grad = g_ref[:, c].astype(F32)
        normed = inv * o_ref[:, c]
        do_ref[:, c] = (inv * (grad * gain_ref[pl.ds(h, 1), :] - normed * cr_ref[...])).astype(BF16)
        gsrc_ref[h] = jnp.sum((grad * normed).reshape(tok // 8, 8, size), axis=0)

    for i in range(half):
        norm_grad(theirs + i)
        b_ls[i] = local_state(theirs + i, q_ref, enter_ref, do_ref)
        l_copy(bwd, b_l_sem, i).start()
        norm_grad(own + i)
        b_lo[i] = local_state(own + i, q_ref, enter_ref, do_ref)
        if i > 0:

            @pl.when(b_head)
            def _():
                chain_step(bwd, bwd_sems, -1, dlow_ref, i - 1)

    @pl.when(b_head)
    def _():
        chain_step(bwd, bwd_sems, -1, dlow_ref, half - 1)

    def gain_copy(j, slot):
        return remote(
            gsrc_ref.at[j], grecv_ref.at[slot], gain_sem.at[0, j], gain_sem.at[1, slot],
            {"seq": j},
        )

    def gain_send(j, carry):
        @pl.when(j != pos)
        def _():
            gain_copy(j, pos).start()

        return carry

    def gain_recv(j, carry):
        @pl.when(j != pos)
        def _():
            gain_copy(j, j).wait_recv()
            gain_copy(j, pos).wait_send()

        return carry

    def put(h):
        c = cols(h)
        return [
            pltpu.make_async_copy(src.at[:, c], dst.at[:, c], out_sem.at[n, h])
            for n, (src, dst) in enumerate(
                ((dq_ref, dq_hbm), (dki_ref, dki_hbm), (dvi_ref, dvi_hbm))
            )
        ]

    def put_state(h):
        return pltpu.make_async_copy(dlow_ref.at[h], dlow_hbm.at[h], out_sem.at[3, h])

    def intra_grad(h, carry):
        c = cols(h)
        top, low = weights(h)
        q0, q1 = q_ref[early, c], q_ref[late, c]
        d0, d1 = do_ref[early, c], do_ref[late, c]
        da_top = (dot(d0, v_ref[early, c], NT) * top).astype(BF16)
        da_low = (dot(d1, v_ref[:, c], NT) * low).astype(BF16)
        enter = decay(h, enter_ref)
        state = low_ref[h]
        dq_ref[early, c] = (
            dot(da_top, k_ref[early, c], NN) + enter[:mid] * dot(d0, state, NT)
        ).astype(BF16)
        dq_ref[late, c] = (
            dot(da_low, k_ref[:, c], NN) + enter[mid:] * dot(d1, state, NT)
        ).astype(BF16)
        dki_ref[early, c] = (dot(da_top, q0, TN) + dot(da_low[:, :mid], q1, TN)).astype(BF16)
        dki_ref[late, c] = dot(da_low[:, mid:], q1, TN).astype(BF16)
        dvi_ref[early, c] = (
            dot(mix_ref[h, 0:mid, 0:mid], d0, TN) + dot(mix_ref[h, mid:tok, 0:mid], d1, TN)
        ).astype(BF16)
        dvi_ref[late, c] = dot(mix_ref[h, mid:tok, mid:tok], d1, TN).astype(BF16)
        for copy in put(h):
            copy.start()
        return carry

    if scatter:
        lax.fori_loop(0, n_seq, gain_send, 0)
    b_before = jnp.minimum((chips - 1 - chip) * BWD_PER_HOP, heads)
    lax.fori_loop(0, b_before, intra_grad, 0)

    def bwd_theirs(i, carry):
        take_partner(bwd, b_s_sem, dlow_ref, i)
        put_state(theirs + i).start()
        return carry

    def bwd_chain(i, carry):
        @pl.when(jnp.logical_not(b_head))
        def _():
            chain_step(bwd, bwd_sems, -1, dlow_ref, i)

        put_state(own + i).start()
        return carry

    lax.fori_loop(0, half, bwd_chain, 0)
    lax.fori_loop(b_before, heads, intra_grad, 0)
    lax.fori_loop(0, half, bwd_theirs, 0)

    if scatter:
        grecv_ref[pos] = gsrc_ref[pos]
        lax.fori_loop(0, n_seq, gain_recv, 0)
        gain_sum = grecv_ref[0]
        for j in range(1, n_seq):
            gain_sum = gain_sum + grecv_ref[j]
        gg_ref[...] = jnp.sum(gain_sum, axis=0, keepdims=True)
    else:
        for h in range(heads):
            gg_ref[h : h + 1, :] = jnp.sum(gsrc_ref[h], axis=0, keepdims=True)
    finish(fwd, fwd_sems, 1)
    finish(bwd, bwd_sems, -1)

    def put_done(h, carry):
        for copy in put(h):
            copy.wait()
        put_state(h).wait()
        return carry

    lax.fori_loop(0, heads, put_done, 0)
    lax.fori_loop(0, n_dp, stat_done, 0)


def shards(queries, keys, values, out_grad, gain, decay_index, bounds):
    tok, width = queries.shape
    heads = decay_index.shape[0]
    size = width // heads
    n_seq, n_dp = lax.axis_size("seq"), lax.axis_size("dp")
    half = heads // 2
    scatter = n_seq == heads
    cfg = (tok, heads, size, n_seq, n_dp, scatter)
    vmem = pl.BlockSpec(memory_space=pltpu.VMEM)
    anywhere = pl.BlockSpec(memory_space=pl.ANY)
    smem = pl.BlockSpec(memory_space=pltpu.SMEM)
    state = pltpu.VMEM((half, size, size), F32)
    dma = pltpu.SemaphoreType.DMA
    chain_sems = [dma((2, half)), dma((2, half * CHUNKS)), dma((2, half * CHUNKS))]
    grads = jax.ShapeDtypeStruct((tok, width), BF16)
    query_part, key_part, value_part, state_grad, gain_part = pl.pallas_call(
        functools.partial(kernel, cfg),
        out_shape=[
            grads,
            grads,
            grads,
            jax.ShapeDtypeStruct((heads, size, size), BF16),
            jax.ShapeDtypeStruct((1 if scatter else heads, size), F32),
        ],
        in_specs=[anywhere] * 4 + [vmem] + [smem] * 2,
        out_specs=[anywhere] * 4 + [vmem],
        scratch_shapes=[pltpu.VMEM((tok, width), BF16)] * 5
        + [
            pltpu.VMEM((heads, 1, tok), F32),
            pltpu.VMEM((2, heads, 1, size), F32),
            pltpu.VMEM((tok, size), F32),
            pltpu.VMEM((tok, size), F32),
            pltpu.VMEM((tok, tok), F32),
            pltpu.VMEM((heads, tok, tok), BF16),
            pltpu.VMEM((tok, width), F32),
            pltpu.VMEM((tok, width), BF16),
            pltpu.VMEM((tok, width), BF16),
            pltpu.VMEM((tok, width), BF16),
            pltpu.VMEM((heads, size, size), BF16),
            pltpu.VMEM((heads, size, size), BF16),
            pltpu.VMEM((tok, size), F32),
            pltpu.VMEM((tok, size), F32),
            pltpu.VMEM((n_dp, 8, tok), F32),
            pltpu.VMEM((heads, 8, size), F32),
            pltpu.VMEM((n_seq, 8, size), F32),
        ]
        + [state] * 14
        + chain_sems * 2
        + [dma((2, n_dp)), dma((2, n_seq)), dma((4,)), dma((4, heads))],
        compiler_params=pltpu.CompilerParams(
            collective_id=0, has_side_effects=True, vmem_limit_bytes=60 * 1024 * 1024
        ),
    )(queries, keys, values, out_grad, gain.reshape(heads, size), decay_index, bounds)
    wide = pl.BlockSpec((tok, FINAL_HEADS * size), lambda j: (0, j))
    gain_spec = pl.BlockSpec(gain_part.shape, lambda j: (0, 0))
    query_grad, key_grad, value_grad, gain_part = pl.pallas_call(
        functools.partial(final_kernel, (tok, size, n_seq)),
        grid=(heads // FINAL_HEADS,),
        out_shape=[grads, grads, grads, jax.ShapeDtypeStruct(gain_part.shape, F32)],
        in_specs=[smem] * 2
        + [wide] * 5
        + [pl.BlockSpec((FINAL_HEADS, size, size), lambda j: (j, 0, 0)), gain_spec],
        out_specs=[wide] * 3 + [gain_spec],
    )(decay_index, bounds, keys, values, query_part, key_part, value_part, state_grad, gain_part)
    if scatter:
        gain_grad = gain_part.reshape(-1)
    else:
        gain_grad = lax.psum_scatter(
            gain_part.reshape(-1), "seq", scatter_dimension=0, tiled=True
        )
    return query_grad, key_grad, value_grad, gain_grad


def solution(mesh):
    return jax.shard_map(
        shards,
        mesh=mesh,
        in_specs=(
            P("seq", "dp"),
            P("seq", "dp"),
            P("seq", "dp"),
            P("seq", "dp"),
            P("dp"),
            P("dp"),
            P(),
        ),
        out_specs=(P("seq", "dp"), P("seq", "dp"), P("seq", "dp"), P(("dp", "seq"))),
        check_vma=False,
    )
```

```python
import functools
import math

import jax
import jax.numpy as jnp
from jax import lax
from jax.experimental import pallas as pl
from jax.experimental.pallas import tpu as pltpu
from jax.sharding import PartitionSpec as P

MESH = pl.DeviceIdType.MESH
F32, BF16 = jnp.float32, jnp.bfloat16
FAR = 1e30
CHUNKS = 4
FWD_PER_HOP = 4
BWD_PER_HOP = 3
FINAL_HEADS = 4

NN = (((1,), (0,)), ((), ()))
NT = (((1,), (1,)), ((), ()))
TN = (((0,), (0,)), ((), ()))


def dot(a, b, dims):
    return lax.dot_general(a, b, dims, preferred_element_type=F32)


def decay_rates(level_int, stream):
    level = level_int.astype(F32)
    lowest = math.log(4.0 / stream)
    slow = -0.25 * jnp.exp(level / 7.0 * math.log(8.0)) / stream
    fast = -jnp.exp(lowest + (level - 8.0) / 7.0 * (math.log(1.0 / 32.0) - lowest))
    return jnp.where(level_int < 8, slow, fast)


def episode_of(bounds_ref, place):
    total = 0
    for b in range(bounds_ref.shape[0]):
        total = total + (bounds_ref[b] <= place).astype(jnp.int32)
    return total


def final_kernel(
    cfg, dec_ref, bounds_ref, k_ref, v_ref, dqi_ref, dki_ref, dvi_ref, dlow_ref, ggi_ref,
    dq_ref, dk_ref, dv_ref, gg_ref,
):
    tok, size, n_seq = cfg
    first = lax.axis_index("seq") * tok
    t_col = lax.broadcasted_iota(jnp.int32, (tok, size), 0)
    same = episode_of(bounds_ref, first + t_col) == episode_of(bounds_ref, first + tok - 1)
    leave_pos = jnp.where(same, tok - 1.0 - t_col.astype(F32), FAR)
    dq_ref[...] = dqi_ref[...]
    gg_ref[...] = ggi_ref[...]
    for u in range(FINAL_HEADS):
        level = jnp.full((1, size), dec_ref[pl.program_id(0) * FINAL_HEADS + u], jnp.int32)
        leave = jnp.exp(decay_rates(level, float(tok * n_seq)) * leave_pos)
        c = slice(u * size, (u + 1) * size)
        state = dlow_ref[u]
        dk_ref[:, c] = (dki_ref[:, c].astype(F32) + leave * dot(v_ref[:, c], state, NT)).astype(BF16)
        dv_ref[:, c] = (dvi_ref[:, c].astype(F32) + leave * dot(k_ref[:, c], state, NN)).astype(BF16)


def kernel(
    cfg,
    q_hbm, k_hbm, v_hbm, g_hbm, gain_ref, dec_ref, bounds_ref,
    dq_hbm, dki_hbm, dvi_hbm, dlow_hbm, gg_ref,
    q_ref, k_ref, v_ref, g_ref, dq_ref,
    rate_ref, pass_ref, enter_ref, leave_ref, dist_ref,
    mix_ref, o_ref, do_ref, dki_ref, dvi_ref, low_ref, dlow_ref,
    sq_ref, cr_ref, stat_ref, gsrc_ref, grecv_ref,
    f_ls, f_lo, f_lr, f_x, f_xs, f_ss, f_sr,
    b_ls, b_lo, b_lr, b_x, b_xs, b_ss, b_sr,
    f_l_sem, f_x_sem, f_s_sem, b_l_sem, b_x_sem, b_s_sem, stat_sem, gain_sem,
    in_sem, out_sem,
):
    tok, heads, size, n_seq, n_dp, scatter = cfg
    half, mid = heads // 2, tok // 2
    rows = size // CHUNKS
    pos, dpi = lax.axis_index("seq"), lax.axis_index("dp")
    core, chip = lax.rem(pos, 2), lax.div(pos, 2)
    chips = n_seq // 2
    partner = chip * 2 + 1 - core
    loads = [
        pltpu.make_async_copy(src, dst, in_sem.at[i])
        for i, (src, dst) in enumerate(
            ((k_hbm, k_ref), (v_hbm, v_ref), (q_hbm, q_ref), (g_hbm, g_ref))
        )
    ]
    for load in loads:
        load.start()
    barrier = pltpu.get_barrier_semaphore()

    def greet(axis, mine):
        def body(j, carry):
            @pl.when(j != mine)
            def _():
                pl.semaphore_signal(barrier, inc=1, device_id={axis: j}, device_id_type=MESH)

            return carry

        return body

    lax.fori_loop(0, n_seq, greet("seq", pos), 0)
    lax.fori_loop(0, n_dp, greet("dp", dpi), 0)

    def cols(h):
        return pl.ds(pl.multiple_of(h * size, size), size)

    def episode(place):
        return episode_of(bounds_ref, place)

    first = pos * tok
    line = lax.broadcasted_iota(jnp.int32, (heads, tok), 0)
    level_int = jnp.zeros((heads, tok), jnp.int32)
    for h in range(heads):
        level_int = jnp.where(line == h, dec_ref[h], level_int)
    rates = decay_rates(level_int, float(tok * n_seq))
    for h in range(heads):
        rate_ref[h] = rates[h : h + 1]
    for c in range(2):
        start = (chip * 2 + c) * tok
        whole = (episode(start + tok - 1) == episode(start - 1)).astype(F32)
        passing = jnp.exp(rates[:, :size] * float(tok)) * whole
        for h in range(heads):
            pass_ref[c, h] = passing[h : h + 1]
    t_col = lax.broadcasted_iota(jnp.int32, (tok, size), 0)
    e_col = episode(first + t_col)
    t_val = t_col.astype(F32)
    enter_ref[...] = jnp.where(e_col == episode(first - 1), t_val + 1.0, FAR)
    leave_ref[...] = jnp.where(e_col == episode(first + tok - 1), tok - 1.0 - t_val, FAR)

    def decay(h, where_ref):
        return jnp.exp(rate_ref[h][:, :size] * where_ref[...])

    def local_state(h, a_ref, where_ref, b_ref):
        scaled = (decay(h, where_ref) * a_ref[:, cols(h)].astype(F32)).astype(BF16)
        return dot(scaled, b_ref[:, cols(h)], TN)

    theirs, own = (1 - core) * half, core * half

    def remote(src, dst, send, recv, target):
        return pltpu.make_async_remote_copy(
            src_ref=src, dst_ref=dst, send_sem=send, recv_sem=recv,
            device_id=target, device_id_type=MESH,
        )

    def l_copy(bufs, sem, i):
        return remote(bufs[0].at[i], bufs[2].at[i], sem.at[0, i], sem.at[1, i], {"seq": partner})

    def x_copy(bufs, sem, i, r, step):
        part = pl.ds(r * rows, rows)
        return remote(
            bufs[4].at[i, part], bufs[3].at[i, part],
            sem.at[0, i * CHUNKS + r], sem.at[1, i * CHUNKS + r], {"seq": pos + 2 * step},
        )

    def s_copy(bufs, sem, i, r):
        part = pl.ds(r * rows, rows)
        return remote(
            bufs[5].at[i, part], bufs[6].at[i, part],
            sem.at[0, i * CHUNKS + r], sem.at[1, i * CHUNKS + r], {"seq": partner},
        )

    def direction(step):
        if step > 0:
            return core, chip > 0, chip < chips - 1
        return 1 - core, chip < chips - 1, chip > 0

    def chain_step(bufs, sems, step, target_ref, i):
        rel, has_up, has_down = direction(step)
        near, distant = (0, 1) if step > 0 else (1, 0)
        l_sem, x_sem, s_sem = sems
        lo, lr, x_in, xs, ss = bufs[1], bufs[2], bufs[3], bufs[4], bufs[5]
        is_near = rel == 0
        h = own + i
        l_copy(bufs, l_sem, i).wait_recv()
        pa, pb = pass_ref[near, h], pass_ref[distant, h]
        for r in range(CHUNKS):
            part = pl.ds(r * rows, rows)

            @pl.when(has_up)
            def _():
                x_copy(bufs, x_sem, i, r, step).wait_recv()

            @pl.when(jnp.logical_not(has_up))
            def _():
                x_in[i, part, :] = jnp.zeros((rows, size), F32)

            x, mine, other = x_in[i, part, :], lo[i, part, :], lr[i, part, :]
            la, lb = jnp.where(is_near, mine, other), jnp.where(is_near, other, mine)
            after = pa * x + la
            xs[i, part, :] = pb * after + lb

            @pl.when(has_down)
            def _():
                x_copy(bufs, x_sem, i, r, step).start()

            ss[i, part, :] = jnp.where(is_near, after, x)
            s_copy(bufs, s_sem, i, r).start()
            target_ref[h, part, :] = jnp.where(is_near, x, after).astype(BF16)

    def take_partner(bufs, s_sem, target_ref, i):
        for r in range(CHUNKS):
            s_copy(bufs, s_sem, i, r).wait_recv()
        target_ref[theirs + i] = bufs[6][i].astype(BF16)

    def finish(bufs, sems, step):
        l_sem, x_sem, s_sem = sems
        has_down = direction(step)[2]

        def body(i, carry):
            l_copy(bufs, l_sem, i).wait_send()
            for r in range(CHUNKS):
                s_copy(bufs, s_sem, i, r).wait_send()

                @pl.when(has_down)
                def _():
                    x_copy(bufs, x_sem, i, r, step).wait_send()

            return carry

        lax.fori_loop(0, half, body, 0)

    fwd = (f_ls, f_lo, f_lr, f_x, f_xs, f_ss, f_sr)
    bwd = (b_ls, b_lo, b_lr, b_x, b_xs, b_ss, b_sr)

    fwd_sems = (f_l_sem, f_x_sem, f_s_sem)
    bwd_sems = (b_l_sem, b_x_sem, b_s_sem)

    f_head, b_head = chip == 0, chip == chips - 1
    loads[0].wait()
    loads[1].wait()
    for i in range(half):
        f_ls[i] = local_state(theirs + i, k_ref, leave_ref, v_ref)
        if i == 0:
            pl.semaphore_wait(barrier, n_seq - 1 + n_dp - 1)
        l_copy(fwd, f_l_sem, i).start()
        f_lo[i] = local_state(own + i, k_ref, leave_ref, v_ref)
        if i > 0:

            @pl.when(f_head)
            def _():
                chain_step(fwd, fwd_sems, 1, low_ref, i - 1)

    @pl.when(f_head)
    def _():
        chain_step(fwd, fwd_sems, 1, low_ref, half - 1)

    loads[2].wait()
    loads[3].wait()

    t_full = lax.broadcasted_iota(jnp.int32, (tok, tok), 0)
    s_full = lax.broadcasted_iota(jnp.int32, (tok, tok), 1)
    e_row = episode(first + lax.broadcasted_iota(jnp.int32, (1, tok), 1))
    e_tall = episode(first + lax.broadcasted_iota(jnp.int32, (tok, 1), 0))
    allowed = (t_full >= s_full) & (e_row == e_tall)
    early, late = pl.ds(0, mid), pl.ds(mid, mid)

    def weights(h):
        rate = rate_ref[h]
        top = jnp.exp(rate[:, :mid] * dist_ref[0:mid, 0:mid])
        low = jnp.exp(rate * dist_ref[mid:tok, :])
        return top, low

    def intra(h, carry):
        c = cols(h)
        top, low = weights(h)
        k_all = k_ref[:, c]
        a_top = (dot(q_ref[early, c], k_ref[early, c], NT) * top).astype(BF16)
        a_low = (dot(q_ref[late, c], k_all, NT) * low).astype(BF16)
        mix_ref[h, 0:mid, 0:mid] = a_top
        mix_ref[h, mid:tok, :] = a_low
        o_ref[early, c] = dot(a_top, v_ref[early, c], NN)
        o_ref[late, c] = dot(a_low, v_ref[:, c], NN)
        return carry

    f_before = jnp.minimum(chip * FWD_PER_HOP, heads)
    f_full = f_before >= heads
    dist_ref[...] = jnp.where(allowed, (t_full - s_full).astype(F32), FAR)
    lax.fori_loop(0, f_before, intra, 0)

    sq_ref[...] = jnp.zeros_like(sq_ref)
    cr_ref[...] = jnp.zeros_like(cr_ref)

    def outputs(h):
        c = cols(h)
        o = o_ref[:, c] + decay(h, enter_ref) * dot(q_ref[:, c], low_ref[h], NN)
        o_ref[:, c] = o
        sq_ref[...] += o * o
        cr_ref[...] += g_ref[:, c].astype(F32) * gain_ref[pl.ds(h, 1), :] * o

    def out_own(i, carry):
        outputs(own + i)
        return carry

    def out_theirs(i, carry):
        take_partner(fwd, f_s_sem, low_ref, i)
        outputs(theirs + i)
        return carry

    def fwd_chain(i, carry):
        chain_step(fwd, fwd_sems, 1, low_ref, i)

        @pl.when(f_full)
        def _():
            out_own(i, 0)

        @pl.when(f_full & (i > 0))
        def _():
            out_theirs(i - 1, 0)

        return carry

    lax.fori_loop(jnp.where(f_head, half, 0), half, fwd_chain, 0)
    lax.fori_loop(f_before, heads, intra, 0)
    lax.fori_loop(jnp.where(f_full, half, 0), half, out_own, 0)
    lax.fori_loop(jnp.where(f_full, half - 1, 0), half, out_theirs, 0)

    sq_row = jnp.sum(jnp.transpose(sq_ref[...]), axis=0, keepdims=True)
    cr_row = jnp.sum(jnp.transpose(cr_ref[...]), axis=0, keepdims=True)
    line8 = lax.broadcasted_iota(jnp.int32, (8, tok), 0)
    stat_ref[dpi] = jnp.where(line8 == 0, sq_row, jnp.where(line8 == 1, cr_row, 0.0))

    def stat_copy(j, slot):
        return remote(
            stat_ref.at[slot], stat_ref.at[slot], stat_sem.at[0, j], stat_sem.at[1, slot],
            {"dp": j},
        )

    def stat_send(j, carry):
        @pl.when(j != dpi)
        def _():
            stat_copy(j, dpi).start()

        return carry

    def stat_recv(j, carry):
        @pl.when(j != dpi)
        def _():
            stat_copy(j, j).wait_recv()

        return carry

    def stat_done(j, carry):
        @pl.when(j != dpi)
        def _():
            stat_copy(j, dpi).wait_send()

        return carry

    lax.fori_loop(0, n_dp, stat_send, 0)
    lax.fori_loop(0, n_dp, stat_recv, 0)
    total = stat_ref[0]
    for j in range(1, n_dp):
        total = total + stat_ref[j]
    features = float(heads * size * n_dp)
    inv_row = lax.rsqrt(total[0:1, :] / features + 1e-06)
    mean_row = inv_row * total[1:2, :] / features
    sq_ref[...] = jnp.transpose(jnp.broadcast_to(inv_row, (size, tok)))
    cr_ref[...] = jnp.transpose(jnp.broadcast_to(mean_row, (size, tok)))

    def norm_grad(h):
        c = cols(h)
        inv = sq_ref[...]
        grad = g_ref[:, c].astype(F32)
        normed = inv * o_ref[:, c]
        do_ref[:, c] = (inv * (grad * gain_ref[pl.ds(h, 1), :] - normed * cr_ref[...])).astype(BF16)
        gsrc_ref[h] = jnp.sum((grad * normed).reshape(tok // 8, 8, size), axis=0)

    for i in range(half):
        norm_grad(theirs + i)
        b_ls[i] = local_state(theirs + i, q_ref, enter_ref, do_ref)
        l_copy(bwd, b_l_sem, i).start()
        norm_grad(own + i)
        b_lo[i] = local_state(own + i, q_ref, enter_ref, do_ref)
        if i > 0:

            @pl.when(b_head)
            def _():
                chain_step(bwd, bwd_sems, -1, dlow_ref, i - 1)

    @pl.when(b_head)
    def _():
        chain_step(bwd, bwd_sems, -1, dlow_ref, half - 1)

    def gain_copy(j, slot):
        return remote(
            gsrc_ref.at[j], grecv_ref.at[slot], gain_sem.at[0, j], gain_sem.at[1, slot],
            {"seq": j},
        )

    def gain_send(j, carry):
        @pl.when(j != pos)
        def _():
            gain_copy(j, pos).start()

        return carry

    def gain_recv(j, carry):
        @pl.when(j != pos)
        def _():
            gain_copy(j, j).wait_recv()
            gain_copy(j, pos).wait_send()

        return carry

    def put(h):
        c = cols(h)
        return [
            pltpu.make_async_copy(src.at[:, c], dst.at[:, c], out_sem.at[n, h])
            for n, (src, dst) in enumerate(
                ((dq_ref, dq_hbm), (dki_ref, dki_hbm), (dvi_ref, dvi_hbm))
            )
        ]

    def put_state(h):
        return pltpu.make_async_copy(dlow_ref.at[h], dlow_hbm.at[h], out_sem.at[3, h])

    def intra_grad(h, carry):
        c = cols(h)
        top, low = weights(h)
        q0, q1 = q_ref[early, c], q_ref[late, c]
        d0, d1 = do_ref[early, c], do_ref[late, c]
        da_top = (dot(d0, v_ref[early, c], NT) * top).astype(BF16)
        da_low = (dot(d1, v_ref[:, c], NT) * low).astype(BF16)
        enter = decay(h, enter_ref)
        state = low_ref[h]
        dq_ref[early, c] = (
            dot(da_top, k_ref[early, c], NN) + enter[:mid] * dot(d0, state, NT)
        ).astype(BF16)
        dq_ref[late, c] = (
            dot(da_low, k_ref[:, c], NN) + enter[mid:] * dot(d1, state, NT)
        ).astype(BF16)
        dki_ref[early, c] = (dot(da_top, q0, TN) + dot(da_low[:, :mid], q1, TN)).astype(BF16)
        dki_ref[late, c] = dot(da_low[:, mid:], q1, TN).astype(BF16)
        dvi_ref[early, c] = (
            dot(mix_ref[h, 0:mid, 0:mid], d0, TN) + dot(mix_ref[h, mid:tok, 0:mid], d1, TN)
        ).astype(BF16)
        dvi_ref[late, c] = dot(mix_ref[h, mid:tok, mid:tok], d1, TN).astype(BF16)
        for copy in put(h):
            copy.start()
        return carry

    if scatter:
        lax.fori_loop(0, n_seq, gain_send, 0)
    b_before = jnp.minimum((chips - 1 - chip) * BWD_PER_HOP, heads)
    lax.fori_loop(0, b_before, intra_grad, 0)

    def bwd_theirs(i, carry):
        take_partner(bwd, b_s_sem, dlow_ref, i)
        put_state(theirs + i).start()
        return carry

    def bwd_chain(i, carry):
        @pl.when(jnp.logical_not(b_head))
        def _():
            chain_step(bwd, bwd_sems, -1, dlow_ref, i)

        put_state(own + i).start()

        @pl.when(i > 0)
        def _():
            bwd_theirs(i - 1, 0)

        return carry

    lax.fori_loop(0, half, bwd_chain, 0)
    lax.fori_loop(b_before, heads, intra_grad, 0)
    bwd_theirs(half - 1, 0)

    if scatter:
        grecv_ref[pos] = gsrc_ref[pos]
        lax.fori_loop(0, n_seq, gain_recv, 0)
        gain_sum = grecv_ref[0]
        for j in range(1, n_seq):
            gain_sum = gain_sum + grecv_ref[j]
        gg_ref[...] = jnp.sum(gain_sum, axis=0, keepdims=True)
    else:
        for h in range(heads):
            gg_ref[h : h + 1, :] = jnp.sum(gsrc_ref[h], axis=0, keepdims=True)
    finish(fwd, fwd_sems, 1)
    finish(bwd, bwd_sems, -1)

    def put_done(h, carry):
        for copy in put(h):
            copy.wait()
        put_state(h).wait()
        return carry

    lax.fori_loop(0, heads, put_done, 0)
    lax.fori_loop(0, n_dp, stat_done, 0)


def shards(queries, keys, values, out_grad, gain, decay_index, bounds):
    tok, width = queries.shape
    heads = decay_index.shape[0]
    size = width // heads
    n_seq, n_dp = lax.axis_size("seq"), lax.axis_size("dp")
    half = heads // 2
    scatter = n_seq == heads
    cfg = (tok, heads, size, n_seq, n_dp, scatter)
    vmem = pl.BlockSpec(memory_space=pltpu.VMEM)
    anywhere = pl.BlockSpec(memory_space=pl.ANY)
    smem = pl.BlockSpec(memory_space=pltpu.SMEM)
    state = pltpu.VMEM((half, size, size), F32)
    dma = pltpu.SemaphoreType.DMA
    chain_sems = [dma((2, half)), dma((2, half * CHUNKS)), dma((2, half * CHUNKS))]
    grads = jax.ShapeDtypeStruct((tok, width), BF16)
    query_part, key_part, value_part, state_grad, gain_part = pl.pallas_call(
        functools.partial(kernel, cfg),
        out_shape=[
            grads,
            grads,
            grads,
            jax.ShapeDtypeStruct((heads, size, size), BF16),
            jax.ShapeDtypeStruct((1 if scatter else heads, size), F32),
        ],
        in_specs=[anywhere] * 4 + [vmem] + [smem] * 2,
        out_specs=[anywhere] * 4 + [vmem],
        scratch_shapes=[pltpu.VMEM((tok, width), BF16)] * 5
        + [
            pltpu.VMEM((heads, 1, tok), F32),
            pltpu.VMEM((2, heads, 1, size), F32),
            pltpu.VMEM((tok, size), F32),
            pltpu.VMEM((tok, size), F32),
            pltpu.VMEM((tok, tok), F32),
            pltpu.VMEM((heads, tok, tok), BF16),
            pltpu.VMEM((tok, width), F32),
            pltpu.VMEM((tok, width), BF16),
            pltpu.VMEM((tok, width), BF16),
            pltpu.VMEM((tok, width), BF16),
            pltpu.VMEM((heads, size, size), BF16),
            pltpu.VMEM((heads, size, size), BF16),
            pltpu.VMEM((tok, size), F32),
            pltpu.VMEM((tok, size), F32),
            pltpu.VMEM((n_dp, 8, tok), F32),
            pltpu.VMEM((heads, 8, size), F32),
            pltpu.VMEM((n_seq, 8, size), F32),
        ]
        + [state] * 14
        + chain_sems * 2
        + [dma((2, n_dp)), dma((2, n_seq)), dma((4,)), dma((4, heads))],
        compiler_params=pltpu.CompilerParams(
            collective_id=0, has_side_effects=True, vmem_limit_bytes=60 * 1024 * 1024
        ),
    )(queries, keys, values, out_grad, gain.reshape(heads, size), decay_index, bounds)
    wide = pl.BlockSpec((tok, FINAL_HEADS * size), lambda j: (0, j))
    gain_spec = pl.BlockSpec(gain_part.shape, lambda j: (0, 0))
    query_grad, key_grad, value_grad, gain_part = pl.pallas_call(
        functools.partial(final_kernel, (tok, size, n_seq)),
        grid=(heads // FINAL_HEADS,),
        out_shape=[grads, grads, grads, jax.ShapeDtypeStruct(gain_part.shape, F32)],
        in_specs=[smem] * 2
        + [wide] * 5
        + [pl.BlockSpec((FINAL_HEADS, size, size), lambda j: (j, 0, 0)), gain_spec],
        out_specs=[wide] * 3 + [gain_spec],
    )(decay_index, bounds, keys, values, query_part, key_part, value_part, state_grad, gain_part)
    if scatter:
        gain_grad = gain_part.reshape(-1)
    else:
        gain_grad = lax.psum_scatter(
            gain_part.reshape(-1), "seq", scatter_dimension=0, tiled=True
        )
    return query_grad, key_grad, value_grad, gain_grad


def solution(mesh):
    return jax.shard_map(
        shards,
        mesh=mesh,
        in_specs=(
            P("seq", "dp"),
            P("seq", "dp"),
            P("seq", "dp"),
            P("seq", "dp"),
            P("dp"),
            P("dp"),
            P(),
        ),
        out_specs=(P("seq", "dp"), P("seq", "dp"), P("seq", "dp"), P(("dp", "seq"))),
        check_vma=False,
    )
```
